128 devices in a mesh: ctx: 16 (over x, y), head: 8 (over z, core).
Axes of the slice: x: 4, y: 4, z: 4, core: 2. Of those that a mesh axis runs over, the one named last changes fastest.
Arguments:
- query_rows: bfloat16 [32768, 8192], P('ctx', 'head'), may hold values from -0.3984375 to 0.3984375
- key_rows: bfloat16 [32768, 8192], P('ctx', 'head'), may hold values from -6 to 6
- value_rows: bfloat16 [32768, 8192], P('ctx', 'head'), may hold values from -6 to 6
- level_weights: float32 [17, 32, 32768], P(None, 'head', 'ctx'), may hold values from 0.2 to 2
Outputs:
- attended: bfloat16 [32768, 8192], P(('ctx', 'head'))
The draws below stay inside these ranges and needn't reach their ends.
All inputs are finite; a program needn't handle non-finite values.
Results may differ from the reference program's by a relative error of at most 0.0049.
Values may be sent and summed in bfloat16 or wider, within the bound.
A program may use at most 192 MiB of HBM per device.

```python
import math
import jax
import jax.numpy as jnp
from jax import lax

HEADS = 32
HDIM = 256
BLK = 512
LEVELS = 17
WIDTH = 8192
TOKENS = 32768


def shard_levels(rng, dims, pieces, smallest, largest):
    loudness = 1.0
    for position, shards_of in pieces:
        draws = jax.random.uniform(jax.random.fold_in(jax.random.fold_in(rng, 6), position), (shards_of,), jnp.float32, smallest / len(pieces), largest / len(pieces))
        loudness = loudness * jnp.repeat(jnp.exp(draws), dims[position] // shards_of).reshape((-1,) + (1,) * (len(dims) - 1 - position))
    return loudness


def noise(rng, extent, deviation, limit, split=(), dtype=jnp.bfloat16):
    values = jax.random.normal(rng, extent, jnp.float32) * deviation
    if len(split) > 0:
        values = shard_levels(rng, extent, split, -0.22, 0.18) * values
    return jnp.clip(values, min=-limit, max=limit).astype(dtype)


def setup_inputs(seed: int = 0) -> dict:
    splits = jax.random.split(jax.random.key(seed), 5)
    return {
        "query_rows": noise(splits[0], (TOKENS, WIDTH), 0.0625, 0.3984375, ((0, 16), (1, 8))),
        "key_rows": noise(splits[1], (TOKENS, WIDTH), 1.0, 6.0, ((0, 16), (1, 8))),
        "value_rows": noise(splits[2], (TOKENS, WIDTH), 1.0, 6.0, ((0, 16), (1, 8))),
        "level_weights": jnp.clip(jnp.exp(math.log(2.0) - 2.3025851 * jax.random.uniform(splits[3], (LEVELS, HEADS, TOKENS), jnp.float32) ** shard_levels(splits[3], (LEVELS, HEADS, TOKENS), ((1, 8), (2, 16)), -0.2, 0.2)), 0.2, 2.0),
    }


def level_grid(size):
    rows_index = lax.broadcasted_iota(jnp.int32, (size, size), 0)
    cols_index = lax.broadcasted_iota(jnp.int32, (size, size), 1)
    xored = jnp.bitwise_xor(rows_index, cols_index)
    grid = jnp.zeros((size, size), jnp.int32)
    for power in range(size.bit_length() - 1):
        grid = grid + (xored >= 2 ** power).astype(jnp.int32)
    return grid, cols_index <= rows_index


def level_scale():
    levels_index = jnp.arange(LEVELS).astype(jnp.float32)
    return jnp.exp2(-0.5 * jnp.maximum(levels_index - 1.0, 0.0))


def reference(query_rows, key_rows, value_rows, level_weights):
    blocks = TOKENS // BLK
    block_bits = BLK.bit_length() - 1
    global_bits = blocks.bit_length() - 1
    highest = lax.Precision.HIGHEST
    scaled = level_weights * level_scale()[:, None, None]
    per_head = scaled.reshape(LEVELS, HEADS, blocks, BLK).transpose(1, 0, 2, 3)

    def split_heads(rows_in):
        return rows_in.reshape(blocks, BLK, HEADS, HDIM).transpose(2, 0, 1, 3)

    grid, causal = level_grid(BLK)
    later_block = jnp.arange(blocks).astype(jnp.int32)[:, None]
    earlier_block = jnp.arange(blocks).astype(jnp.int32)[None, :]

    def one_head(inputs):
        queries_head, keys_head, values_head, weights_head = inputs
        query_float = queries_head.astype(jnp.float32)
        key_float = keys_head.astype(jnp.float32)
        value_float = values_head.astype(jnp.float32)
        scores = jnp.einsum("ntd,nsd->nts", query_float, key_float, precision=highest)
        weight_table = jnp.zeros((blocks, BLK, BLK), jnp.float32)
        for level in range(block_bits + 1):
            weight_table = weight_table + jnp.where(grid == level, weights_head[level][:, :, None], jnp.float32(0.0))
        weight_table = jnp.where(causal, weight_table, jnp.float32(0.0))
        weighted = (scores * weight_table).astype(jnp.bfloat16)
        output_sum = jnp.einsum("nts,nse->nte", weighted.astype(jnp.float32), value_float, precision=highest)
        states = jnp.einsum("ntd,nte->nde", key_float, value_float, precision=highest)
        for global_bit in range(global_bits):
            chosen = ((earlier_block < later_block) & (jnp.right_shift(jnp.bitwise_xor(later_block, earlier_block), global_bit) == 1)).astype(jnp.float32)
            level_state = jnp.einsum("nm,mde->nde", chosen, states, precision=highest).astype(jnp.bfloat16)
            product = jnp.einsum("ntd,nde->nte", query_float, level_state.astype(jnp.float32), precision=highest)
            output_sum = output_sum + product * weights_head[block_bits + 1 + global_bit][:, :, None]
        return output_sum

    result = lax.map(one_head, (split_heads(query_rows), split_heads(key_rows), split_heads(value_rows), per_head))
    return result.transpose(1, 2, 0, 3).reshape(TOKENS, HEADS * HDIM).astype(jnp.bfloat16)
```

```python
import jax
import jax.numpy as jnp
from jax import lax
from jax.experimental import pallas as pl
from jax.experimental.pallas import tpu as pltpu
from jax.sharding import PartitionSpec as P

MESH = pl.DeviceIdType.MESH
F32 = jnp.float32
BF16 = jnp.bfloat16
BLK = 512
HEADS = 4
DIM = 256
TOKENS = 2048
BLOCKS = TOKENS // BLK
SHARE = 256
TILE = 128
USED_LEVELS = 16
NT = (((1,), (1,)), ((), ()))
TN = (((0,), (0,)), ((), ()))
PEERS = ((2, 0), (2, 1), (1, 0), (1, 1), (3, 0), (3, 1), (0, 1))


def dot(a, b, dims=(((1,), (0,)), ((), ()))):
    return lax.dot_general(a, b, dims, preferred_element_type=F32)


def kernel(
    q_hbm, k_hbm, v_hbm, w_hbm, out_ref,
    q_all, k_all, v_all, w_all, w_rows, w_cols, grid_ref, probs, acc,
    local_states, own, y_send, y_recv, x_send, x_recv, remote, staged,
    in_sem, w_sem, ys_sem, yr_sem, xs_sem, xr_sem, os_sem, or_sem,
):
    ctx = lax.axis_index("ctx")
    me = lax.axis_index("head")
    x, y = ctx // 4, ctx % 4
    z, core = me // 2, me % 2

    barrier = pltpu.get_barrier_semaphore()
    for step in range(1, 4):
        for there in (x * 4 + (y + step) % 4, ((x + step) % 4) * 4 + y):
            pl.semaphore_signal(barrier, inc=1, device_id={"ctx": there}, device_id_type=MESH)
    for dz, dc in PEERS:
        there = ((z + dz) % 4) * 2 + (core + dc) % 2
        pl.semaphore_signal(barrier, inc=1, device_id={"head": there}, device_id_type=MESH)

    def fetch(which, j):
        source = (q_hbm, k_hbm, v_hbm)[which]
        target = (q_all, k_all, v_all)[which]
        columns = pl.ds(pl.multiple_of(j * DIM, DIM), DIM)
        return pltpu.make_async_copy(source.at[:, columns], target.at[j], in_sem.at[which, j])

    fetch(1, 0).start()
    fetch(2, 0).start()
    fetch_w = pltpu.make_async_copy(w_hbm, w_all, w_sem)
    fetch(0, 0).start()
    fetch_w.start()
    for j in range(1, HEADS):
        for which in (1, 2, 0):
            fetch(which, j).start()

    def y_copy(j, step):
        return pltpu.make_async_remote_copy(
            src_ref=y_send.at[j],
            dst_ref=y_recv.at[j, step - 1],
            send_sem=ys_sem.at[j, step - 1],
            recv_sem=yr_sem.at[j, step - 1],
            device_id={"ctx": x * 4 + (y + step) % 4},
            device_id_type=MESH,
        )

    def x_copy(j, step):
        return pltpu.make_async_remote_copy(
            src_ref=x_send.at[j],
            dst_ref=x_recv.at[j, step - 1],
            send_sem=xs_sem.at[j, step - 1],
            recv_sem=xr_sem.at[j, step - 1],
            device_id={"ctx": ((x + step) % 4) * 4 + y},
            device_id_type=MESH,
        )

    def out_copy(j, index):
        dz, dc = PEERS[index]
        there = ((z + dz) % 4) * 2 + (core + dc) % 2
        columns = pl.ds(pl.multiple_of((me * HEADS + j) * DIM, DIM), DIM)
        rows = pl.ds(pl.multiple_of(there * SHARE, SHARE), SHARE)
        return pltpu.make_async_remote_copy(
            src_ref=staged.at[j, rows],
            dst_ref=out_ref.at[:, columns],
            send_sem=os_sem.at[j, index],
            recv_sem=or_sem.at[j, index],
            device_id={"head": there},
            device_id_type=MESH,
        )

    def state_rows(j, index, count):
        return pl.ds(pl.multiple_of((j * 3 + index) * DIM, DIM), count * DIM)

    def make_states(j):
        fetch(1, j).wait()
        fetch(2, j).wait()
        parts = []
        for b in range(BLOCKS):
            rows = pl.ds(b * BLK, BLK)
            parts.append(dot(k_all[j, rows, :], v_all[j, rows, :], TN))
        pair = parts[0] + parts[1]
        for index, state in enumerate((parts[0], pair, parts[2])):
            local_states[state_rows(j, index, 1), :] = state.astype(BF16)
        total = pair + (parts[2] + parts[3])
        own[...] = total
        y_send[j] = total.astype(BF16)

    def send_y(j):
        for step in range(1, 4):
            y_copy(j, step).start()

    def make_weights(j):
        for head in range(HEADS):

            @pl.when(j == head)
            def _():
                for level in range(USED_LEVELS):
                    scale = 2.0 ** (-0.5 * max(level - 1.0, 0.0))
                    w_rows[level : level + 1, :] = w_all[level, head : head + 1, :] * scale

        for part in range(TOKENS // TILE):
            rows = slice(part * TILE, (part + 1) * TILE)
            w_cols[rows, :USED_LEVELS] = w_rows[:, rows].T

    def local_block(j, b):
        base = b * BLK
        half = BLK // 2
        queries = q_all[j, pl.ds(base, BLK), :]
        low = dot(queries, k_all[j, pl.ds(base, half), :], NT)
        high = dot(queries[half:], k_all[j, pl.ds(base + half, half), :], NT)

        def weight(level, start, size):
            return w_cols[base + start : base + start + size, level : level + 1]

        grid = grid_ref[...]
        for tile in range(BLK // TILE):
            start = tile * TILE
            table = jnp.zeros((TILE, TILE), F32)
            for level in range(8):
                table = jnp.where(grid == level, weight(level, start, TILE), table)
            source = low if tile < 2 else high
            first = start % half
            diagonal = source[first : first + TILE, first : first + TILE] * table
            probs[start : start + TILE, start : start + TILE] = diagonal.astype(BF16)
            if tile % 2 == 1:
                beside = source[first : first + TILE, :TILE] * weight(8, start, TILE)
                probs[start : start + TILE, start - TILE : start] = beside.astype(BF16)
        probs[half:, :half] = (low[half:] * weight(9, half, half)).astype(BF16)

        values = v_all[j, pl.ds(base, BLK), :]
        top = dot(probs[:half, :half], values[:half])
        bottom = dot(probs[half:, :], values)

        acc[base : base + half, :] = top
        acc[base + half : base + BLK, :] = bottom
        if b > 0:
            rows = slice(base, base + BLK)
            queries = q_all[j, rows, :].astype(F32)
            bits = [bit for bit in (1, 0) if (b >> bit) & 1]
            left = [(queries * w_cols[rows, 10 + bit : 11 + bit]).astype(BF16) for bit in bits]
            right = local_states[state_rows(j, (0, 0, 1, 1)[b], len(bits)), :]
            acc[rows, :] = acc[rows, :] + dot(jnp.concatenate(left, axis=1), right)

    def exchange_x(j):
        for step in range(1, 4):
            y_copy(j, step).wait_recv()
        total = own[...]
        for step in range(3):
            total = total + y_recv[j, step].astype(F32)
        x_send[j] = total.astype(BF16)
        for step in range(1, 4):

            @pl.when(x + step < 4)
            def _():
                x_copy(j, step).start()

        remote[: 2 * DIM, :] = jnp.zeros((2 * DIM, DIM), BF16)

        @pl.when(y % 2 == 1)
        def _():
            remote[:DIM, :] = y_recv[j, 0]

        @pl.when(y >= 2)
        def _():
            pair = y_recv[j, y - 1].astype(F32) + y_recv[j, y - 2].astype(F32)
            remote[DIM : 2 * DIM, :] = pair.astype(BF16)

    def finish_x(j):
        for step in range(1, 4):

            @pl.when(x >= step)
            def _():
                x_copy(j, step).wait_recv()

        remote[2 * DIM :, :] = jnp.zeros((2 * DIM, DIM), BF16)

        @pl.when(x % 2 == 1)
        def _():
            remote[2 * DIM : 3 * DIM, :] = x_recv[j, 0]

        @pl.when(x >= 2)
        def _():
            pair = x_recv[j, x - 1].astype(F32) + x_recv[j, x - 2].astype(F32)
            remote[3 * DIM :, :] = pair.astype(BF16)

    def finish_share(j, there):
        rows = pl.ds(pl.multiple_of(there * SHARE, SHARE), SHARE)
        queries = q_all[j, rows, :].astype(F32)
        weights = w_cols[rows, :]
        left = jnp.concatenate(
            [(queries * weights[:, 12 + bit : 13 + bit]).astype(BF16) for bit in range(4)], axis=1
        )
        return (acc[rows, :] + dot(left, remote[...])).astype(BF16)

    make_states(0)
    pl.semaphore_wait(barrier, 13)
    send_y(0)

    rows_index = lax.broadcasted_iota(jnp.int32, (TILE, TILE), 0)
    cols_index = lax.broadcasted_iota(jnp.int32, (TILE, TILE), 1)
    xored = jnp.bitwise_xor(rows_index, cols_index)
    grid = jnp.zeros((TILE, TILE), jnp.int32)
    for power in range(7):
        grid = grid + (xored >= 2**power).astype(jnp.int32)
    grid_ref[...] = jnp.where(cols_index <= rows_index, grid, 99)
    probs[...] = jnp.zeros((BLK, BLK), BF16)
    fetch_w.wait()

    @pl.loop(0, HEADS)
    def _(j):
        make_weights(j)
        fetch(0, j).wait()
        local_block(j, 0)
        local_block(j, 1)
        exchange_x(j)

        @pl.when(j + 1 < HEADS)
        def _():
            make_states(j + 1)
            send_y(j + 1)

        local_block(j, 2)
        local_block(j, 3)
        finish_x(j)
        for index, (dz, dc) in enumerate(PEERS):
            there = ((z + dz) % 4) * 2 + (core + dc) % 2
            rows = pl.ds(pl.multiple_of(there * SHARE, SHARE), SHARE)
            staged[j, rows, :] = finish_share(j, there)
            out_copy(j, index).start()
        columns = pl.ds(pl.multiple_of((me * HEADS + j) * DIM, DIM), DIM)
        out_ref[:, columns] = finish_share(j, me)

    @pl.loop(0, HEADS)
    def _(j):
        for step in range(1, 4):
            y_copy(j, step).wait_send()

            @pl.when(x + step < 4)
            def _():
                x_copy(j, step).wait_send()

        for index in range(len(PEERS)):
            out_copy(j, index).wait()


def store(in_ref, out_ref, sem):
    copy = pltpu.make_async_copy(in_ref, out_ref, sem)
    copy.start()
    copy.wait()


def local(query_rows, key_rows, value_rows, level_weights):
    hbm = pl.BlockSpec(memory_space=pl.ANY)
    vmem = pl.BlockSpec(memory_space=pltpu.VMEM)
    dma = pltpu.SemaphoreType.DMA
    width = HEADS * DIM * 8
    gathered = pl.pallas_call(
        kernel,
        out_shape=jax.ShapeDtypeStruct((SHARE, width), BF16),
        in_specs=[hbm] * 4,
        out_specs=vmem,
        scratch_shapes=[
            pltpu.VMEM((HEADS, TOKENS, DIM), BF16),
            pltpu.VMEM((HEADS, TOKENS, DIM), BF16),
            pltpu.VMEM((HEADS, TOKENS, DIM), BF16),
            pltpu.VMEM(level_weights.shape, F32),
            pltpu.VMEM((USED_LEVELS, TOKENS), F32),
            pltpu.VMEM((TOKENS, TILE), F32),
            pltpu.VMEM((TILE, TILE), jnp.int32),
            pltpu.VMEM((BLK, BLK), BF16),
            pltpu.VMEM((TOKENS, DIM), F32),
            pltpu.VMEM((HEADS * 3 * DIM, DIM), BF16),
            pltpu.VMEM((DIM, DIM), F32),
            pltpu.VMEM((HEADS, DIM, DIM), BF16),
            pltpu.VMEM((HEADS, 3, DIM, DIM), BF16),
            pltpu.VMEM((HEADS, DIM, DIM), BF16),
            pltpu.VMEM((HEADS, 3, DIM, DIM), BF16),
            pltpu.VMEM((4 * DIM, DIM), BF16),
            pltpu.VMEM((HEADS, TOKENS, DIM), BF16),
            dma((3, HEADS)),
            dma,
            dma((HEADS, 3)),
            dma((HEADS, 3)),
            dma((HEADS, 3)),
            dma((HEADS, 3)),
            dma((HEADS, len(PEERS))),
            dma((HEADS, len(PEERS))),
        ],
        compiler_params=pltpu.CompilerParams(
            collective_id=0, has_side_effects=True, vmem_limit_bytes=48 * 2**20
        ),
    )(query_rows, key_rows, value_rows, level_weights)
    return pl.pallas_call(
        store,
        out_shape=jax.ShapeDtypeStruct((SHARE, width), BF16),
        in_specs=[vmem],
        out_specs=hbm,
        scratch_shapes=[dma],
    )(gathered)


def solution(mesh):
    in_specs = (P("ctx", "head"), P("ctx", "head"), P("ctx", "head"), P(None, "head", "ctx"))
    out_specs = P(("ctx", "head"), None)
    return jax.shard_map(local, mesh=mesh, in_specs=in_specs, out_specs=out_specs, check_vma=False)
```

```python
import jax
import jax.numpy as jnp
from jax import lax
from jax.experimental import pallas as pl
from jax.experimental.pallas import tpu as pltpu
from jax.sharding import PartitionSpec as P

MESH = pl.DeviceIdType.MESH
F32 = jnp.float32
BF16 = jnp.bfloat16
BLK = 512
HEADS = 4
DIM = 256
TOKENS = 2048
BLOCKS = TOKENS // BLK
SHARE = 256
TILE = 128
USED_LEVELS = 16
NT = (((1,), (1,)), ((), ()))
TN = (((0,), (0,)), ((), ()))
HALF = DIM // 2
CHUNKS = 2
PIECE = DIM // CHUNKS
PEERS = ((2, 0), (2, 1), (1, 0), (1, 1), (3, 0), (3, 1), (0, 1))


def dot(a, b, dims=(((1,), (0,)), ((), ()))):
    return lax.dot_general(a, b, dims, preferred_element_type=F32)


def kernel(
    q_hbm, k_hbm, v_hbm, w_hbm, out_ref,
    q_all, k_all, v_all, w_all, w_rows, w_cols, grid_ref, probs, acc,
    local_states, y_send, y_recv, x_send, x_recv, remote, staged,
    in_sem, w_sem, ys_sem, yr_sem, xs_sem, xr_sem, os_sem, or_sem,
):
    ctx = lax.axis_index("ctx")
    me = lax.axis_index("head")
    x, y = ctx // 4, ctx % 4
    z, core = me // 2, me % 2

    barrier = pltpu.get_barrier_semaphore()
    for step in range(1, 4):
        for there in (x * 4 + (y + step) % 4, ((x + step) % 4) * 4 + y):
            pl.semaphore_signal(barrier, inc=1, device_id={"ctx": there}, device_id_type=MESH)
    for dz, dc in PEERS:
        there = ((z + dz) % 4) * 2 + (core + dc) % 2
        pl.semaphore_signal(barrier, inc=1, device_id={"head": there}, device_id_type=MESH)

    def fetch(which, j):
        source = (q_hbm, k_hbm, v_hbm)[which]
        target = (q_all, k_all, v_all)[which]
        columns = pl.ds(pl.multiple_of(j * DIM, DIM), DIM)
        return pltpu.make_async_copy(source.at[:, columns], target.at[j], in_sem.at[which, j])

    fetch(1, 0).start()
    fetch(2, 0).start()
    fetch_w = pltpu.make_async_copy(w_hbm, w_all, w_sem)

    def fetch_rest():
        fetch(0, 0).start()
        fetch_w.start()
        for j in range(1, HEADS):
            for which in (1, 2, 0):
                fetch(which, j).start()

    def at(index, start=0, size=DIM):
        return pl.ds(pl.multiple_of(index * DIM + start, PIECE), size)

    def y_copy(j, half, chunk, step):
        index = j * 2 + half
        return pltpu.make_async_remote_copy(
            src_ref=y_send.at[at(index, chunk * PIECE, PIECE)],
            dst_ref=y_recv.at[at(index * 3 + step - 1, chunk * PIECE, PIECE)],
            send_sem=ys_sem.at[index, chunk * 3 + step - 1],
            recv_sem=yr_sem.at[index, chunk * 3 + step - 1],
            device_id={"ctx": x * 4 + (y + step) % 4},
            device_id_type=MESH,
        )

    def x_copy(j, half, chunk, step):
        index = j * 2 + half
        return pltpu.make_async_remote_copy(
            src_ref=x_send.at[at(index, chunk * PIECE, PIECE)],
            dst_ref=x_recv.at[at(index * 3 + step - 1, chunk * PIECE, PIECE)],
            send_sem=xs_sem.at[index, chunk * 3 + step - 1],
            recv_sem=xr_sem.at[index, chunk * 3 + step - 1],
            device_id={"ctx": ((x + step) % 4) * 4 + y},
            device_id_type=MESH,
        )

    def out_columns(j):
        return pl.ds(pl.multiple_of((me * HEADS + j) * DIM, DIM), DIM)

    def out_copy(j, index):
        dz, dc = PEERS[index]
        there = ((z + dz) % 4) * 2 + (core + dc) % 2
        rows = pl.ds(pl.multiple_of(there * SHARE, SHARE), SHARE)
        return pltpu.make_async_remote_copy(
            src_ref=staged.at[j, rows],
            dst_ref=out_ref.at[:, out_columns(j)],
            send_sem=os_sem.at[j, index],
            recv_sem=or_sem.at[j, index],
            device_id={"head": there},
            device_id_type=MESH,
        )

    def make_states(j):
        fetch(1, j).wait()
        fetch(2, j).wait()
        parts = []
        for b in range(BLOCKS):
            rows = pl.ds(b * BLK, BLK)
            parts.append(dot(k_all[j, rows, :], v_all[j, rows, :], TN))
        pair = parts[0] + parts[1]
        zero = jnp.zeros((DIM, DIM), BF16)
        first, second, joint = parts[0].astype(BF16), parts[2].astype(BF16), pair.astype(BF16)
        for b, states in enumerate(((zero, zero), (first, zero), (zero, joint), (second, joint))):
            for bit in range(2):
                start = pl.multiple_of(((j * BLOCKS + b) * 2 + bit) * DIM, DIM)
                local_states[pl.ds(start, DIM), :] = states[bit]
        total = pair + (parts[2] + parts[3])
        for half in range(2):
            y_send[at(j * 2 + half), :] = total[:, half * HALF : (half + 1) * HALF].astype(BF16)

    def send_y(j):
        for half in range(2):
            for chunk in range(CHUNKS):
                for step in range(1, 4):
                    y_copy(j, half, chunk, step).start()

    def make_weights(j):
        for head in range(HEADS):

            @pl.when(j == head)
            def _():
                for level in range(USED_LEVELS):
                    scale = 2.0 ** (-0.5 * max(level - 1.0, 0.0))
                    w_rows[level : level + 1, :] = w_all[level, head : head + 1, :] * scale

        for part in range(TOKENS // TILE):
            rows = slice(part * TILE, (part + 1) * TILE)
            w_cols[rows, :USED_LEVELS] = w_rows[:, rows].T

    def local_block(j, b):
        half = BLK // 2

        def rows(start, size):
            return pl.ds(pl.multiple_of(b * BLK + start, TILE), size)

        queries = q_all[j, rows(0, BLK), :]
        low = dot(queries, k_all[j, rows(0, half), :], NT)
        high = dot(queries[half:], k_all[j, rows(half, half), :], NT)

        def weight(level, start, size):
            return w_cols[rows(start, size), level : level + 1]

        grid = grid_ref[...]
        for tile in range(BLK // TILE):
            start = tile * TILE
            table = jnp.zeros((TILE, TILE), F32)
            for level in range(8):
                table = jnp.where(grid == level, weight(level, start, TILE), table)
            source = low if tile < 2 else high
            first = start % half
            diagonal = source[first : first + TILE, first : first + TILE] * table
            probs[start : start + TILE, start : start + TILE] = diagonal.astype(BF16)
            if tile % 2 == 1:
                beside = source[first : first + TILE, :TILE] * weight(8, start, TILE)
                probs[start : start + TILE, start - TILE : start] = beside.astype(BF16)
        probs[half:, :half] = (low[half:] * weight(9, half, half)).astype(BF16)

        values = v_all[j, rows(0, BLK), :]
        top = dot(probs[:half, :half], values[:half])
        bottom = dot(probs[half:, :], values)
        wide = queries.astype(F32)
        left = [(wide * weight(10 + bit, 0, BLK)).astype(BF16) for bit in range(2)]
        start = pl.multiple_of((j * BLOCKS + b) * 2 * DIM, DIM)
        right = local_states[pl.ds(start, 2 * DIM), :]
        product = dot(jnp.concatenate(left, axis=1), right)
        acc[rows(0, half), :] = top + product[:half]
        acc[rows(half, half), :] = bottom + product[half:]

    def exchange_x(j, half):
        index = j * 2 + half
        for chunk in range(CHUNKS):
            start = chunk * PIECE
            total = y_send[at(index, start, PIECE), :].astype(F32)
            for step in range(1, 4):
                y_copy(j, half, chunk, step).wait_recv()
                arrived = y_recv[at(index * 3 + step - 1, start, PIECE), :]
                total = total + arrived.astype(F32)
            x_send[at(index, start, PIECE), :] = total.astype(BF16)
            for step in range(1, 4):

                @pl.when(x + step < 4)
                def _():
                    x_copy(j, half, chunk, step).start()

        combine(half, 0, y, y_recv, index)

    def combine(half, bit, place, received, index):
        columns = slice(half * HALF, (half + 1) * HALF)
        first = slice(bit * DIM, (bit + 1) * DIM)
        second = slice((bit + 1) * DIM, (bit + 2) * DIM)
        remote[first, columns] = jnp.zeros((DIM, HALF), BF16)
        remote[second, columns] = jnp.zeros((DIM, HALF), BF16)

        @pl.when(place % 2 == 1)
        def _():
            remote[first, columns] = received[at(index * 3), :]

        @pl.when(place >= 2)
        def _():
            pair = received[at(index * 3 + place - 1), :].astype(F32)
            pair = pair + received[at(index * 3 + place - 2), :].astype(F32)
            remote[second, columns] = pair.astype(BF16)

    def finish_x(j, half):
        for chunk in range(CHUNKS):
            for step in range(1, 4):

                @pl.when(x >= step)
                def _():
                    x_copy(j, half, chunk, step).wait_recv()

        combine(half, 2, x, x_recv, j * 2 + half)

    def finish_share(j, there):
        rows = pl.ds(pl.multiple_of(there * SHARE, SHARE), SHARE)
        queries = q_all[j, rows, :].astype(F32)
        weights = w_cols[rows, :]
        left = jnp.concatenate(
            [(queries * weights[:, 12 + bit : 13 + bit]).astype(BF16) for bit in range(4)], axis=1
        )
        return (acc[rows, :] + dot(left, remote[...])).astype(BF16)

    def finish(j, distance):
        for index, (dz, dc) in enumerate(PEERS):
            if dz == distance:
                there = ((z + dz) % 4) * 2 + (core + dc) % 2
                rows = pl.ds(pl.multiple_of(there * SHARE, SHARE), SHARE)
                staged[j, rows, :] = finish_share(j, there)
                out_copy(j, index).start()
        if distance == 0:
            out_ref[:, out_columns(j)] = finish_share(j, me)

    make_states(0)
    fetch_rest()
    pl.semaphore_wait(barrier, 13)
    send_y(0)

    rows_index = lax.broadcasted_iota(jnp.int32, (TILE, TILE), 0)
    cols_index = lax.broadcasted_iota(jnp.int32, (TILE, TILE), 1)
    xored = jnp.bitwise_xor(rows_index, cols_index)
    grid = jnp.zeros((TILE, TILE), jnp.int32)
    for power in range(7):
        grid = grid + (xored >= 2**power).astype(jnp.int32)
    grid_ref[...] = jnp.where(cols_index <= rows_index, grid, 99)
    probs[...] = jnp.zeros((BLK, BLK), BF16)
    fetch_w.wait()

    @pl.loop(0, HEADS)
    def _(j):
        make_weights(j)
        fetch(0, j).wait()
        local_block(j, (z + 2) % 4)
        exchange_x(j, 0)
        exchange_x(j, 1)
        local_block(j, (z + 1) % 4)
        local_block(j, (z + 3) % 4)
        finish_x(j, 0)
        finish_x(j, 1)
        finish(j, 2)
        finish(j, 1)
        finish(j, 3)

        @pl.when(j == 0)
        def _():
            make_states(1)
            send_y(1)

        local_block(j, z)
        finish(j, 0)

        @pl.when(j + 2 < HEADS)
        def _():
            make_states(j + 2)
            send_y(j + 2)

    @pl.loop(0, HEADS)
    def _(j):
        for half in range(2):
            for chunk in range(CHUNKS):
                for step in range(1, 4):
                    y_copy(j, half, chunk, step).wait_send()

                    @pl.when(x + step < 4)
                    def _():
                        x_copy(j, half, chunk, step).wait_send()

        for index in range(len(PEERS)):
            out_copy(j, index).wait()


def store(in_ref, out_ref, sem):
    copy = pltpu.make_async_copy(in_ref, out_ref, sem)
    copy.start()
    copy.wait()


def local(query_rows, key_rows, value_rows, level_weights):
    hbm = pl.BlockSpec(memory_space=pl.ANY)
    vmem = pl.BlockSpec(memory_space=pltpu.VMEM)
    dma = pltpu.SemaphoreType.DMA
    width = HEADS * DIM * 8
    gathered = pl.pallas_call(
        kernel,
        out_shape=jax.ShapeDtypeStruct((SHARE, width), BF16),
        in_specs=[hbm] * 4,
        out_specs=vmem,
        scratch_shapes=[
            pltpu.VMEM((HEADS, TOKENS, DIM), BF16),
            pltpu.VMEM((HEADS, TOKENS, DIM), BF16),
            pltpu.VMEM((HEADS, TOKENS, DIM), BF16),
            pltpu.VMEM(level_weights.shape, F32),
            pltpu.VMEM((USED_LEVELS, TOKENS), F32),
            pltpu.VMEM((TOKENS, TILE), F32),
            pltpu.VMEM((TILE, TILE), jnp.int32),
            pltpu.VMEM((BLK, BLK), BF16),
            pltpu.VMEM((TOKENS, DIM), F32),
            pltpu.VMEM((HEADS * BLOCKS * 2 * DIM, DIM), BF16),
            pltpu.VMEM((HEADS * 2 * DIM, HALF), BF16),
            pltpu.VMEM((HEADS * 6 * DIM, HALF), BF16),
            pltpu.VMEM((HEADS * 2 * DIM, HALF), BF16),
            pltpu.VMEM((HEADS * 6 * DIM, HALF), BF16),
            pltpu.VMEM((4 * DIM, DIM), BF16),
            pltpu.VMEM((HEADS, TOKENS, DIM), BF16),
            dma((3, HEADS)),
            dma,
            dma((HEADS * 2, CHUNKS * 3)),
            dma((HEADS * 2, CHUNKS * 3)),
            dma((HEADS * 2, CHUNKS * 3)),
            dma((HEADS * 2, CHUNKS * 3)),
            dma((HEADS, len(PEERS))),
            dma((HEADS, len(PEERS))),
        ],
        compiler_params=pltpu.CompilerParams(
            collective_id=0, has_side_effects=True, vmem_limit_bytes=96 * 2**19
        ),
    )(query_rows, key_rows, value_rows, level_weights)
    return pl.pallas_call(
        store,
        out_shape=jax.ShapeDtypeStruct((SHARE, width), BF16),
        in_specs=[hbm],
        out_specs=hbm,
        scratch_shapes=[dma],
        compiler_params=pltpu.CompilerParams(vmem_limit_bytes=2**20),
    )(gathered)


def solution(mesh):
    in_specs = (P("ctx", "head"), P("ctx", "head"), P("ctx", "head"), P(None, "head", "ctx"))
    out_specs = P(("ctx", "head"), None)
    return jax.shard_map(local, mesh=mesh, in_specs=in_specs, out_specs=out_specs, check_vma=False)
```

```python
import jax
import jax.numpy as jnp
from jax import lax
from jax.experimental import pallas as pl
from jax.experimental.pallas import tpu as pltpu
from jax.sharding import PartitionSpec as P

MESH = pl.DeviceIdType.MESH
F32 = jnp.float32
BF16 = jnp.bfloat16
BLK = 512
HEADS = 4
DIM = 256
TOKENS = 2048
BLOCKS = TOKENS // BLK
SHARE = 256
TILE = 128
USED_LEVELS = 16
NT = (((1,), (1,)), ((), ()))
TN = (((0,), (0,)), ((), ()))
HALF = DIM // 2
CHUNKS = 2
PIECE = DIM // CHUNKS
PEERS = ((2, 0), (2, 1), (1, 0), (1, 1), (3, 0), (3, 1), (0, 1))


def dot(a, b, dims=(((1,), (0,)), ((), ()))):
    return lax.dot_general(a, b, dims, preferred_element_type=F32)


def kernel(
    q_hbm, k_hbm, v_hbm, w_hbm, out_ref,
    q_all, k_all, v_all, w_all, w_rows, w_cols, grid_ref, probs, acc,
    local_states, y_send, y_recv, x_send, x_recv, remote, staged,
    in_sem, w_sem, ys_sem, yr_sem, xs_sem, xr_sem, os_sem, or_sem,
):
    ctx = lax.axis_index("ctx")
    me = lax.axis_index("head")
    x, y = ctx // 4, ctx % 4
    z, core = me // 2, me % 2

    barrier = pltpu.get_barrier_semaphore()
    for step in range(1, 4):
        for there in (x * 4 + (y + step) % 4, ((x + step) % 4) * 4 + y):
            pl.semaphore_signal(barrier, inc=1, device_id={"ctx": there}, device_id_type=MESH)
    for dz, dc in PEERS:
        there = ((z + dz) % 4) * 2 + (core + dc) % 2
        pl.semaphore_signal(barrier, inc=1, device_id={"head": there}, device_id_type=MESH)

    def fetch(which, j):
        source = (q_hbm, k_hbm, v_hbm)[which]
        target = (q_all, k_all, v_all)[which]
        columns = pl.ds(pl.multiple_of(j * DIM, DIM), DIM)
        return pltpu.make_async_copy(source.at[:, columns], target.at[j], in_sem.at[which, j])

    fetch(1, 0).start()
    fetch(2, 0).start()
    fetch_w = pltpu.make_async_copy(w_hbm, w_all, w_sem)
    fetch_w.start()
    fetch(0, 0).start()

    def fetch_rest():
        for j in range(1, HEADS):
            for which in (1, 2, 0):
                fetch(which, j).start()

    def at(index, start=0, size=DIM):
        return pl.ds(pl.multiple_of(index * DIM + start, PIECE), size)

    def y_copy(j, half, chunk, step):
        index = j * 2 + half
        return pltpu.make_async_remote_copy(
            src_ref=y_send.at[at(index, chunk * PIECE, PIECE)],
            dst_ref=y_recv.at[at(index * 3 + step - 1, chunk * PIECE, PIECE)],
            send_sem=ys_sem.at[index, chunk * 3 + step - 1],
            recv_sem=yr_sem.at[index, chunk * 3 + step - 1],
            device_id={"ctx": x * 4 + (y + step) % 4},
            device_id_type=MESH,
        )

    def x_copy(j, half, chunk, step):
        index = j * 2 + half
        return pltpu.make_async_remote_copy(
            src_ref=x_send.at[at(index, chunk * PIECE, PIECE)],
            dst_ref=x_recv.at[at(index * 3 + step - 1, chunk * PIECE, PIECE)],
            send_sem=xs_sem.at[index, chunk * 3 + step - 1],
            recv_sem=xr_sem.at[index, chunk * 3 + step - 1],
            device_id={"ctx": ((x + step) % 4) * 4 + y},
            device_id_type=MESH,
        )

    def out_columns(j):
        return pl.ds(pl.multiple_of((me * HEADS + j) * DIM, DIM), DIM)

    def out_copy(j, index):
        dz, dc = PEERS[index]
        there = ((z + dz) % 4) * 2 + (core + dc) % 2
        rows = pl.ds(pl.multiple_of(there * SHARE, SHARE), SHARE)
        return pltpu.make_async_remote_copy(
            src_ref=staged.at[j, rows],
            dst_ref=out_ref.at[:, out_columns(j)],
            send_sem=os_sem.at[j, index],
            recv_sem=or_sem.at[j, index],
            device_id={"head": there},
            device_id_type=MESH,
        )

    def make_states(j):
        fetch(1, j).wait()
        fetch(2, j).wait()
        parts = []
        for b in range(BLOCKS):
            rows = pl.ds(b * BLK, BLK)
            parts.append(dot(k_all[j, rows, :], v_all[j, rows, :], TN))
        pair = parts[0] + parts[1]
        zero = jnp.zeros((DIM, DIM), BF16)
        first, second, joint = parts[0].astype(BF16), parts[2].astype(BF16), pair.astype(BF16)
        for b, states in enumerate(((zero, zero), (first, zero), (zero, joint), (second, joint))):
            for bit in range(2):
                start = pl.multiple_of(((j * BLOCKS + b) * 2 + bit) * DIM, DIM)
                local_states[pl.ds(start, DIM), :] = states[bit]
        total = pair + (parts[2] + parts[3])
        for half in range(2):
            y_send[at(j * 2 + half), :] = total[:, half * HALF : (half + 1) * HALF].astype(BF16)

    def send_y(j):
        for half in range(2):
            for chunk in range(CHUNKS):
                for step in range(1, 4):
                    y_copy(j, half, chunk, step).start()

    def make_weights(j):
        for head in range(HEADS):

            @pl.when(j == head)
            def _():
                for level in range(USED_LEVELS):
                    scale = 2.0 ** (-0.5 * max(level - 1.0, 0.0))
                    w_rows[level : level + 1, :] = w_all[level, head : head + 1, :] * scale

        for part in range(TOKENS // TILE):
            rows = slice(part * TILE, (part + 1) * TILE)
            w_cols[rows, :USED_LEVELS] = w_rows[:, rows].T

    def local_block(j, b):
        half = BLK // 2

        def rows(start, size):
            return pl.ds(pl.multiple_of(b * BLK + start, TILE), size)

        queries = q_all[j, rows(0, BLK), :]
        low = dot(queries, k_all[j, rows(0, half), :], NT)
        high = dot(queries[half:], k_all[j, rows(half, half), :], NT)

        def weight(level, start, size):
            return w_cols[rows(start, size), level : level + 1]

        grid = grid_ref[...]
        for tile in range(BLK // TILE):
            start = tile * TILE
            table = jnp.zeros((TILE, TILE), F32)
            for level in range(8):
                table = jnp.where(grid == level, weight(level, start, TILE), table)
            source = low if tile < 2 else high
            first = start % half
            diagonal = source[first : first + TILE, first : first + TILE] * table
            probs[start : start + TILE, start : start + TILE] = diagonal.astype(BF16)
            if tile % 2 == 1:
                beside = source[first : first + TILE, :TILE] * weight(8, start, TILE)
                probs[start : start + TILE, start - TILE : start] = beside.astype(BF16)
        probs[half:, :half] = (low[half:] * weight(9, half, half)).astype(BF16)

        values = v_all[j, rows(0, BLK), :]
        top = dot(probs[:half, :half], values[:half])
        bottom = dot(probs[half:, :], values)
        wide = queries.astype(F32)
        left = [(wide * weight(10 + bit, 0, BLK)).astype(BF16) for bit in range(2)]
        start = pl.multiple_of((j * BLOCKS + b) * 2 * DIM, DIM)
        right = local_states[pl.ds(start, 2 * DIM), :]
        product = dot(jnp.concatenate(left, axis=1), right)
        acc[rows(0, half), :] = top + product[:half]
        acc[rows(half, half), :] = bottom + product[half:]

    def exchange_x(j, half):
        index = j * 2 + half
        for chunk in range(CHUNKS):
            start = chunk * PIECE
            total = y_send[at(index, start, PIECE), :].astype(F32)
            for step in range(1, 4):
                y_copy(j, half, chunk, step).wait_recv()
                arrived = y_recv[at(index * 3 + step - 1, start, PIECE), :]
                total = total + arrived.astype(F32)
            x_send[at(index, start, PIECE), :] = total.astype(BF16)
            for step in range(1, 4):

                @pl.when(x + step < 4)
                def _():
                    x_copy(j, half, chunk, step).start()

        combine(half, 0, y, y_recv, index)

    def combine(half, bit, place, received, index):
        columns = slice(half * HALF, (half + 1) * HALF)
        first = slice(bit * DIM, (bit + 1) * DIM)
        second = slice((bit + 1) * DIM, (bit + 2) * DIM)
        remote[first, columns] = jnp.zeros((DIM, HALF), BF16)
        remote[second, columns] = jnp.zeros((DIM, HALF), BF16)

        @pl.when(place % 2 == 1)
        def _():
            remote[first, columns] = received[at(index * 3), :]

        @pl.when(place >= 2)
        def _():
            pair = received[at(index * 3 + place - 1), :].astype(F32)
            pair = pair + received[at(index * 3 + place - 2), :].astype(F32)
            remote[second, columns] = pair.astype(BF16)

    def finish_x(j, half):
        for chunk in range(CHUNKS):
            for step in range(1, 4):

                @pl.when(x >= step)
                def _():
                    x_copy(j, half, chunk, step).wait_recv()

        combine(half, 2, x, x_recv, j * 2 + half)

    def finish_share(j, there):
        rows = pl.ds(pl.multiple_of(there * SHARE, SHARE), SHARE)
        queries = q_all[j, rows, :].astype(F32)
        weights = w_cols[rows, :]
        left = jnp.concatenate(
            [(queries * weights[:, 12 + bit : 13 + bit]).astype(BF16) for bit in range(4)], axis=1
        )
        return (acc[rows, :] + dot(left, remote[...])).astype(BF16)

    def finish(j, distance):
        for index, (dz, dc) in enumerate(PEERS):
            if dz == distance:
                there = ((z + dz) % 4) * 2 + (core + dc) % 2
                rows = pl.ds(pl.multiple_of(there * SHARE, SHARE), SHARE)
                staged[j, rows, :] = finish_share(j, there)
                out_copy(j, index).start()
        if distance == 0:
            out_ref[:, out_columns(j)] = finish_share(j, me)

    make_states(0)
    fetch_rest()
    pl.semaphore_wait(barrier, 13)
    send_y(0)

    rows_index = lax.broadcasted_iota(jnp.int32, (TILE, TILE), 0)
    cols_index = lax.broadcasted_iota(jnp.int32, (TILE, TILE), 1)
    xored = jnp.bitwise_xor(rows_index, cols_index)
    grid = jnp.zeros((TILE, TILE), jnp.int32)
    for power in range(7):
        grid = grid + (xored >= 2**power).astype(jnp.int32)
    grid_ref[...] = jnp.where(cols_index <= rows_index, grid, 99)
    probs[...] = jnp.zeros((BLK, BLK), BF16)
    fetch_w.wait()

    @pl.loop(0, HEADS)
    def _(j):
        make_weights(j)
        fetch(0, j).wait()
        local_block(j, (z + 2) % 4)
        exchange_x(j, 0)
        exchange_x(j, 1)
        local_block(j, (z + 1) % 4)
        local_block(j, (z + 3) % 4)
        finish_x(j, 0)
        finish_x(j, 1)
        finish(j, 2)
        finish(j, 1)
        finish(j, 3)

        @pl.when(j == 0)
        def _():
            make_states(1)
            send_y(1)

        local_block(j, z)
        finish(j, 0)

        @pl.when(j + 2 < HEADS)
        def _():
            make_states(j + 2)
            send_y(j + 2)

    @pl.loop(0, HEADS)
    def _(j):
        for half in range(2):
            for chunk in range(CHUNKS):
                for step in range(1, 4):
                    y_copy(j, half, chunk, step).wait_send()

                    @pl.when(x + step < 4)
                    def _():
                        x_copy(j, half, chunk, step).wait_send()

        for index in range(len(PEERS)):
            out_copy(j, index).wait()


def store(in_ref, out_ref, sem):
    copy = pltpu.make_async_copy(in_ref, out_ref, sem)
    copy.start()
    copy.wait()


def local(query_rows, key_rows, value_rows, level_weights):
    hbm = pl.BlockSpec(memory_space=pl.ANY)
    vmem = pl.BlockSpec(memory_space=pltpu.VMEM)
    dma = pltpu.SemaphoreType.DMA
    width = HEADS * DIM * 8
    gathered = pl.pallas_call(
        kernel,
        out_shape=jax.ShapeDtypeStruct((SHARE, width), BF16),
        in_specs=[hbm] * 3 + [pl.BlockSpec(memory_space=pltpu.HBM)],
        out_specs=vmem,
        scratch_shapes=[
            pltpu.VMEM((HEADS, TOKENS, DIM), BF16),
            pltpu.VMEM((HEADS, TOKENS, DIM), BF16),
            pltpu.VMEM((HEADS, TOKENS, DIM), BF16),
            pltpu.VMEM(level_weights.shape, F32),
            pltpu.VMEM((USED_LEVELS, TOKENS), F32),
            pltpu.VMEM((TOKENS, TILE), F32),
            pltpu.VMEM((TILE, TILE), jnp.int32),
            pltpu.VMEM((BLK, BLK), BF16),
            pltpu.VMEM((TOKENS, DIM), F32),
            pltpu.VMEM((HEADS * BLOCKS * 2 * DIM, DIM), BF16),
            pltpu.VMEM((HEADS * 2 * DIM, HALF), BF16),
            pltpu.VMEM((HEADS * 6 * DIM, HALF), BF16),
            pltpu.VMEM((HEADS * 2 * DIM, HALF), BF16),
            pltpu.VMEM((HEADS * 6 * DIM, HALF), BF16),
            pltpu.VMEM((4 * DIM, DIM), BF16),
            pltpu.VMEM((HEADS, TOKENS, DIM), BF16),
            dma((3, HEADS)),
            dma,
            dma((HEADS * 2, CHUNKS * 3)),
            dma((HEADS * 2, CHUNKS * 3)),
            dma((HEADS * 2, CHUNKS * 3)),
            dma((HEADS * 2, CHUNKS * 3)),
            dma((HEADS, len(PEERS))),
            dma((HEADS, len(PEERS))),
        ],
        compiler_params=pltpu.CompilerParams(
            collective_id=0, has_side_effects=True, vmem_limit_bytes=96 * 2**19
        ),
    )(query_rows, key_rows, value_rows, pltpu.with_memory_space_constraint(level_weights, pltpu.HBM))
    return pl.pallas_call(
        store,
        out_shape=jax.ShapeDtypeStruct((SHARE, width), BF16),
        in_specs=[hbm],
        out_specs=hbm,
        scratch_shapes=[dma],
        compiler_params=pltpu.CompilerParams(vmem_limit_bytes=2**20),
    )(gathered)


def solution(mesh):
    in_specs = (P("ctx", "head"), P("ctx", "head"), P("ctx", "head"), P(None, "head", "ctx"))
    out_specs = P(("ctx", "head"), None)
    return jax.shard_map(local, mesh=mesh, in_specs=in_specs, out_specs=out_specs, check_vma=False)
```
